128 devices in a mesh: gz: 16 (over y_lo, x, core), gy: 8 (over z, y_hi).
Axes of the slice: x: 4, y: 4 (y_hi: 2, y_lo: 2; y = y_hi * 2 + y_lo), z: 4, core: 2. Of those that a mesh axis runs over, the one named last changes fastest.
Arguments:
- fields: bfloat16 [6, 128, 256, 256], P(None, 'gz', 'gy'), may hold values from -13 to 13
- target: bfloat16 [128, 64, 128, 128], P(None, 'gz', 'gy'), may hold values from -6 to 6
- conv_weight: bfloat16 [64, 162], replicated, may hold values from -0.5 to 0.5
- conv_bias: float32 [64], replicated, may hold values from -3 to 3
- down_weight: bfloat16 [128, 512], replicated, may hold values from -0.25 to 0.25
- down_bias: float32 [128], replicated, may hold values from -3 to 3
Outputs:
- out_field: bfloat16 [128, 64, 128, 128], P(None, 'gz', 'gy')
- sensitivity: float32 [6, 128, 256, 256], P(None, 'gz', 'gy')
- grad_conv: float32 [64, 162], replicated
- grad_conv_bias: float32 [64], replicated
- grad_down: float32 [128, 512], P('gz')
- grad_down_bias: float32 [128], replicated
- loss: float32 [], replicated
The draws below stay inside these ranges and needn't reach their ends.
All inputs are finite; a program needn't handle non-finite values.
Results may differ from the reference program's by a relative error of at most 0.0046.
Values may be sent and summed in bfloat16 or wider, within the bound.
A program may use at most 192 MiB of HBM per device.

```python
import math
import jax
import jax.numpy as jnp
from jax import lax

C_IN = 6
HID = 64
OUT = 128
NX = 256
NZ = 128
NY = 256
CELLS2 = 1048576


def draw_fields(key, part):
    key_base = jax.random.fold_in(key, 11)
    key_phase = jax.random.fold_in(key, 23)
    phases = jax.random.uniform(key_phase, (2,), minval=0.0, maxval=2.0 * math.pi)
    z_pos = jnp.arange(NZ, dtype=jnp.float32)[:, None]
    y_pos = jnp.arange(NY, dtype=jnp.float32)[None, :]
    waves = jnp.sin(2.0 * math.pi * z_pos / NZ + phases[0]) + jnp.sin(2.0 * math.pi * y_pos / NY + phases[1])
    base_draw = jnp.clip(jax.random.normal(key_base, (C_IN, NZ, NY, NX)), -4.0, 4.0)
    amplitude = jnp.exp(0.55 * waves)
    return (base_draw * amplitude[None, :, :, None]).astype(jnp.bfloat16)


def block_levels(stream_key, shape, cuts, least, top_value):
    level, own = 1.0, jax.random.fold_in(stream_key, 6)
    for dim, shards_of in cuts:
        draws = jnp.exp(jax.random.uniform(jax.random.fold_in(own, dim), (shards_of,), jnp.float32, least / len(cuts), top_value / len(cuts)))
        level = level * jnp.repeat(draws, shape[dim] // shards_of).reshape([-1 if axis == dim else 1 for axis in range(len(shape))])
    return level


def bell_draw(key, extent, scale, limit, cuts=(), held_as=jnp.bfloat16):
    drawn = jax.random.normal(key, extent, jnp.float32) * scale
    if len(cuts) > 0:
        drawn = block_levels(key, extent, cuts, -0.22, 0.18) * drawn
    return jnp.clip(drawn, min=-limit, max=limit).astype(held_as)


def setup_inputs(seed: int = 0) -> dict:
    seeds = jax.random.split(jax.random.key(seed), 7)
    return {
        "fields": draw_fields(jax.random.fold_in(seeds[6], 71), 0),
        "target": bell_draw(seeds[1], (OUT, NZ // 2, NY // 2, NX // 2), 1.0, 6.0, ((1, 16), (2, 8))),
        "conv_weight": bell_draw(seeds[2], (HID, C_IN * 27), (C_IN * 27) ** -0.5, 0.5),
        "conv_bias": bell_draw(seeds[3], (HID,), 0.5, 3.0, (), jnp.float32),
        "down_weight": bell_draw(seeds[4], (OUT, HID * 8), (HID * 8) ** -0.5, 0.25),
        "down_bias": bell_draw(seeds[5], (OUT,), 0.5, 3.0, (), jnp.float32),
    }


gelu_scale = 0.7978845608028654
gelu_cubic = 0.044715


def gelu_parts(inputs):
    inner_arg = gelu_scale * (inputs + gelu_cubic * inputs * inputs * inputs)
    tangent = jnp.tanh(inner_arg)
    result = 0.5 * inputs * (1.0 + tangent)
    slopes = 0.5 * (1.0 + tangent) + 0.5 * inputs * (1.0 - tangent * tangent) * gelu_scale * (1.0 + 3.0 * gelu_cubic * inputs * inputs)
    return result, slopes


def to_blocks(hidden):
    channels, planes_count, row_count, col_count = hidden.shape
    split = hidden.reshape(channels, 2, row_count // 2, 2, col_count // 2, 2)
    return split.transpose(0, 1, 3, 5, 2, 4).reshape(channels * 8, (row_count // 2) * (col_count // 2))


def from_blocks(blocks, channels, row_count, col_count):
    split = blocks.reshape(channels, 2, 2, 2, row_count // 2, col_count // 2)
    return split.transpose(0, 1, 4, 2, 5, 3).reshape(channels, 2, row_count, col_count)


def column_block(planes):
    pieces = []
    for off_z in range(3):
        for off_y in range(3):
            for off_x in range(3):
                shifted = planes[:, off_z:off_z + 2]
                shifted = jnp.roll(shifted, 1 - off_y, axis=2)
                shifted = jnp.roll(shifted, 1 - off_x, axis=3)
                pieces.append(shifted)
    stacked = jnp.stack(pieces, axis=1)
    return stacked.reshape(C_IN * 27, 2 * NY * NX)


def reference(fields, target, conv_weight, conv_bias, down_weight, down_bias):
    plane_offsets = jnp.arange(4, dtype=jnp.int32)

    def pair_step(state_tuple, pair_index):
        grad_conv, grad_cbias, grad_down, grad_dbias, square_sum, sensitivity = state_tuple
        plane_index = (2 * pair_index - 1 + plane_offsets) % NZ
        planes = jnp.take(fields, plane_index, axis=1)
        columns = column_block(planes)
        pre_act = jnp.dot(conv_weight, columns, preferred_element_type=jnp.float32) + conv_bias[:, None]
        activated, slopes = gelu_parts(pre_act)
        hidden = activated.astype(jnp.bfloat16)
        blocks = to_blocks(hidden.reshape(HID, 2, NY, NX))
        output = jnp.dot(down_weight, blocks, preferred_element_type=jnp.float32) + down_bias[:, None]
        wanted = lax.dynamic_index_in_dim(target, pair_index, 1, keepdims=False).reshape(OUT, -1).astype(jnp.float32)
        diff_value = output - wanted
        grad_out = diff_value.astype(jnp.bfloat16)
        grad_down = grad_down + jnp.dot(grad_out, blocks.T, preferred_element_type=jnp.float32)
        grad_dbias = grad_dbias + jnp.sum(diff_value, axis=1)
        back_hidden = jnp.dot(down_weight.T, grad_out, preferred_element_type=jnp.float32)
        back_hidden = from_blocks(back_hidden, HID, NY, NX).reshape(HID, 2 * NY * NX)
        grad_pre = (back_hidden * slopes).astype(jnp.bfloat16)
        grad_conv = grad_conv + jnp.dot(grad_pre, columns.T, preferred_element_type=jnp.float32)
        grad_cbias = grad_cbias + jnp.sum(grad_pre.astype(jnp.float32), axis=1)
        square_sum = square_sum + jnp.sum(diff_value * diff_value)
        spread = jnp.dot(conv_weight.T, grad_pre, preferred_element_type=jnp.float32).reshape(C_IN, 3, 3, 3, 2, NY, NX)
        window = jnp.zeros((C_IN, 4, NY, NX), jnp.float32)
        for off_z in range(3):
            for off_y in range(3):
                for off_x in range(3):
                    shifted = jnp.roll(spread[:, off_z, off_y, off_x], off_y - 1, axis=2)
                    shifted = jnp.roll(shifted, off_x - 1, axis=3)
                    window = window.at[:, off_z:off_z + 2].add(shifted)
        sensitivity = sensitivity.at[:, plane_index].add(window)
        new_state = (grad_conv, grad_cbias, grad_down, grad_dbias, square_sum, sensitivity)
        return new_state, output.astype(jnp.bfloat16).reshape(OUT, NY // 2, NX // 2)

    start_state = (jnp.zeros((HID, C_IN * 27), jnp.float32), jnp.zeros((HID,), jnp.float32),
                   jnp.zeros((OUT, HID * 8), jnp.float32), jnp.zeros((OUT,), jnp.float32),
                   jnp.zeros((), jnp.float32), jnp.zeros((C_IN, NZ, NY, NX), jnp.float32))
    final_state, outputs = lax.scan(pair_step, start_state, jnp.arange(NZ // 2, dtype=jnp.int32))
    grad_conv, grad_cbias, grad_down, grad_dbias, square_sum, sensitivity = final_state
    out_field = jnp.transpose(outputs, (1, 0, 2, 3))
    return (out_field, sensitivity, grad_conv / CELLS2, grad_cbias / CELLS2,
            grad_down / CELLS2, grad_dbias / CELLS2, square_sum / (OUT * CELLS2))
```

```python
import functools
import jax
import jax.numpy as jnp
from jax import lax
from jax.experimental import pallas as pl
from jax.experimental.pallas import tpu as pltpu
from jax.sharding import PartitionSpec as P

f32, bf16 = jnp.float32, jnp.bfloat16
MESH = pl.DeviceIdType.MESH
C, NZ, NY, NX = 6, 8, 32, 256
HID, OUT = 64, 128
TZ, TY = NZ + 2, NY + 2
HX = NX // 2
ROWS = 4
CELLS = ROWS * HX
SCALE = 0.7978845608028654
CUBIC = 0.044715
NT = (((1,), (1,)), ((), ()))
VMEM = pl.BlockSpec(memory_space=pltpu.VMEM)


def dot(a, b):
    return jnp.dot(a, b, preferred_element_type=f32)


def dot_nt(a, b):
    return lax.dot_general(a, b, NT, preferred_element_type=f32)


def iota(shape, dim):
    return lax.broadcasted_iota(jnp.int32, shape, dim)


def one_hot(mask):
    return jnp.where(mask, 1.0, 0.0)


def split_matrix():
    lane = iota((NX, 4 * HX), 1)
    want = lax.rem(2 * lax.rem(lane, HX) + lane // HX - 1 + NX, NX)
    return one_hot(iota((NX, 4 * HX), 0) == want).astype(bf16)


def tap_matrix(cols):
    lane = iota((C * 27, cols), 1)
    a, b = lane // 128, lax.rem(lane // 32, 4)
    ch, c = lax.rem(lane // 4, 8), lax.rem(lane, 4)
    ok = (a < 3) & (b < 3) & (c < 3) & (ch < C)
    want = jnp.where(ok, ch * 27 + 9 * a + 3 * b + c, -1)
    return one_hot(iota((C * 27, cols), 0) == want)


def column(row, n):
    eye = iota((n, n), 0) == iota((n, n), 1)
    return jnp.sum(jnp.where(eye, jnp.broadcast_to(row, (n, n)), 0.0), axis=1, keepdims=True)


def halves(x):
    hi = x.astype(bf16)
    return hi, (x - hi.astype(f32)).astype(bf16)


def compute_kernel(
    fields, zlo, zhi, ylo, yhi, corners, target, conv_w, conv_b, down_w, down_b,
    out_ref, sens, sz, sy, sc, gd, gc_out,
    split, wide, tiles, tgt, outs, wb, wbt, wdt, wtmp, db, pre, hid, gp, gc, acc, dsum, sqsum, ytmp,
):
    split[...] = split_matrix()

    def spread_rows(value, start, count, stride):
        parts = dot(value, split[...])
        for ch in range(C):
            for dx in range(4):
                wide[pl.ds(start + ch * 4 + dx, count, stride=stride), :] = parts[
                    ch * count : (ch + 1) * count, dx * HX : (dx + 1) * HX
                ]

    def plane(z, carry):
        spread_rows(fields[:, z].reshape(C * NY, NX), ((z + 1) * TY + 1) * 32, NY, 32)
        return carry

    lax.fori_loop(0, NZ, plane, 0)
    spread_rows(zlo[...].reshape(C * NY, NX), 32, NY, 32)
    spread_rows(zhi[...].reshape(C * NY, NX), ((NZ + 1) * TY + 1) * 32, NY, 32)
    spread_rows(ylo[...], TY * 32, NZ, TY * 32)
    spread_rows(yhi[...], (TY + NY + 1) * 32, NZ, TY * 32)
    for k in range(4):
        tile = (k // 2) * (NZ + 1) * TY + (k % 2) * (NY + 1)
        parts = dot(corners[k].astype(bf16), split[...])
        for dx in range(4):
            wide[pl.ds(tile * 32 + dx, 8, stride=4), :] = parts[:, dx * HX : (dx + 1) * HX]

    def cast_tiles(i, carry):
        rows = wide[pl.ds(pl.multiple_of(i * 320, 32), 320), :]
        pad = lax.rem(iota((320, HX), 0), 32) >= 24
        tiles[pl.ds(pl.multiple_of(i * 320, 32), 320), :] = jnp.where(pad, 1.0, rows).astype(bf16)
        return carry

    lax.fori_loop(0, TZ * TY // 10, cast_tiles, 0)

    def cast_target(i, carry):
        at = pl.ds(pl.multiple_of(i * 256, 256), 256)
        tgt[at, :] = target[at, :].astype(f32)
        return carry

    lax.fori_loop(0, OUT * 64 // 256, cast_target, 0)

    taps = tap_matrix(512).astype(bf16)
    base = dot(conv_w[...], taps)
    bias = column(conv_b[...], HID)
    b_hi = bias.astype(bf16).astype(f32)
    b_mid = (bias - b_hi).astype(bf16).astype(f32)
    b_lo = bias - b_hi - b_mid
    lane = iota((HID, 512), 1)
    for par in range(8):
        shift = (par // 4) * 128 + (par // 2 % 2) * 32 + par % 2
        moved = pltpu.roll(base, shift, 1) if shift else base
        moved = jnp.where(lane == 24, b_hi, moved)
        moved = jnp.where(lane == 25, b_mid, moved)
        moved = jnp.where(lane == 26, b_lo, moved)
        for q in range(4):
            wtmp[q, pl.ds(par, HID, stride=8), :] = moved[:, q * 128 : (q + 1) * 128]
    for q in range(4):
        wb[:, q * 128 : (q + 1) * 128] = wtmp[q].astype(bf16)
    row = iota((384, 512), 0)
    keep = one_hot(iota((384, 512), 1) == (row // 24) * 32 + lax.rem(row, 24)).astype(bf16)
    wbt[...] = dot_nt(keep, wb[...]).astype(bf16)
    eye = one_hot(iota((512, 512), 0) == iota((512, 512), 1)).astype(bf16)
    wdt[...] = dot_nt(eye, down_w[...]).astype(bf16)
    db[...] = jnp.broadcast_to(column(down_b[...], OUT), (OUT, HX))

    gd[...] = jnp.zeros_like(gd)
    gc[...] = jnp.zeros_like(gc)
    dsum[...] = jnp.zeros_like(dsum)
    sqsum[...] = jnp.zeros_like(sqsum)

    def clear(i, carry):
        acc[pl.ds(pl.multiple_of(i * 240, 8), 240), :] = jnp.zeros((240, HX), f32)
        return carry

    lax.fori_loop(0, TZ * TY // 10, clear, 0)

    def chunk(i, carry):
        per = 16 // ROWS
        zc = i // per
        y0 = lax.rem(i, per) * ROWS

        def window():
            cols = []
            for r in range(ROWS):
                parts = []
                for dz in range(4):
                    at = ((2 * zc + dz) * TY + 2 * (y0 + r)) * 32
                    parts.append(tiles[pl.ds(pl.multiple_of(at, 64), 128), :])
                cols.append(jnp.concatenate(parts, axis=0))
            return jnp.concatenate(cols, axis=1)

        pre[...] = dot(wb[...], window())
        for m in range(0, 512, 16):
            x = pre[m : m + 16, :]
            x2 = x * x
            t = jnp.tanh(x * (x2 * (SCALE * CUBIC) + SCALE))
            u = 0.5 * t + 0.5
            h = x * u
            hid[m : m + 16, :] = h.astype(bf16)
            pre[m : m + 16, :] = u + (h - h * u) * (x2 * (6 * SCALE * CUBIC) + 2 * SCALE)
        output = dot(down_w[...], hid[...])
        go, ds, sq = [], 0.0, 0.0
        for r in range(ROWS):
            at = pl.ds(zc * 16 + y0 + r, OUT, stride=64)
            value = output[:, r * HX : (r + 1) * HX] + db[...]
            outs[at, :] = value
            diff = value - tgt[at, :]
            ds = ds + diff
            sq = sq + diff * diff
            go.append(diff.astype(bf16))
        dsum[...] += ds
        sqsum[...] += sq
        go = jnp.concatenate(go, axis=1)
        gd[...] += dot_nt(go, hid[...])
        back = dot(wdt[...], go)
        gp[...] = (back * pre[...]).astype(bf16)
        grad = dot_nt(gp[...], window())
        for q in range(4):
            gc[q * 512 : (q + 1) * 512, :] += grad[:, q * 128 : (q + 1) * 128]
        spread = dot(wbt[...], gp[...])
        for dz in range(4):
            for k in range(2 * ROWS + 2):
                total = None
                for r in range(ROWS):
                    dy = k - 2 * r
                    if 0 <= dy < 4:
                        m = (dz * 4 + dy) * 24
                        piece = spread[m : m + 24, r * HX : (r + 1) * HX]
                        total = piece if total is None else total + piece
                at = ((2 * zc + dz) * TY + 2 * y0 + k) * 24
                at = pl.ds(pl.multiple_of(at, 8), 24)
                acc[at, :] += total
        return carry

    lax.fori_loop(0, 64 // ROWS, chunk, 0)

    def cast_out(i, carry):
        at = pl.ds(pl.multiple_of(i * 256, 256), 256)
        out_ref[at, :] = outs[at, :].astype(bf16)
        return carry

    lax.fori_loop(0, OUT * 64 // 256, cast_out, 0)

    def join(rows):
        hi, lo = halves(jnp.concatenate(rows, axis=1))
        return dot_nt(hi, split[...]) + dot_nt(lo, split[...])

    def gather(start, count, stride):
        parts = []
        for dx in range(4):
            pieces = [acc[pl.ds(start + ch * 4 + dx, count, stride=stride), :] for ch in range(C)]
            parts.append(jnp.concatenate(pieces, axis=0))
        return join(parts)

    def sens_plane(z, carry):
        value = gather(((z + 1) * TY + 1) * 24, NY, 24)
        for ch in range(C):
            at = pl.multiple_of(ch * NZ * NY + z * NY, NY)
            sens[pl.ds(at, NY), :] = value[ch * NY : (ch + 1) * NY]
        return carry

    lax.fori_loop(0, NZ, sens_plane, 0)
    sz[0] = gather(24, NY, 24).astype(bf16)
    sz[1] = gather(((NZ + 1) * TY + 1) * 24, NY, 24).astype(bf16)
    sy[0] = gather(TY * 24, NZ, TY * 24).astype(bf16)
    sy[1] = gather((TY + NY + 1) * 24, NZ, TY * 24).astype(bf16)
    ytmp[...] = jnp.zeros_like(ytmp)
    for k in range(4):
        tile = (k // 2) * (NZ + 1) * TY + (k % 2) * (NY + 1)
        ytmp[0:24, :] = acc[tile * 24 : tile * 24 + 24, :]
        sc[k] = join([ytmp[pl.ds(dx, 8, stride=4), :] for dx in range(4)])

    total = None
    for par in range(8):
        shift = (par // 4) * 128 + (par // 2 % 2) * 32 + par % 2
        part = jnp.concatenate(
            [gc[pl.ds(q * 512 + par, HID, stride=8), :] for q in range(4)], axis=1
        )
        part = pltpu.roll(part, 512 - shift, 1) if shift else part
        total = part if total is None else total + part
    total = total[:, :384]
    lane = iota((HID, 384), 1)
    dcol = jnp.sum(dsum[...], axis=1, keepdims=True)
    scol = jnp.sum(sqsum[...], axis=1, keepdims=True)
    total = jnp.where(lane == 28, dcol[:HID], total)
    total = jnp.where(lane == 29, dcol[HID:], total)
    total = jnp.where(lane == 30, scol[:HID] + scol[HID:], total)
    gc_out[...] = total


def compute(fields, halo, target, conv_w, conv_b, down_w, down_b):
    shapes = [
        ((OUT * 64, HX), bf16),
        ((C * NZ * NY, NX), f32),
        ((2, C * NY, NX), bf16),
        ((2, C * NZ, NX), bf16),
        ((4, 8, NX), f32),
        ((OUT, 512), f32),
        ((HID, 384), f32),
    ]
    scratch = [
        ((NX, 4 * HX), bf16),
        ((TZ * TY * 32, HX), f32),
        ((TZ * TY * 32, HX), bf16),
        ((OUT * 64, HX), f32),
        ((OUT * 64, HX), f32),
        ((512, 512), bf16),
        ((384, 512), bf16),
        ((512, OUT), bf16),
        ((4, 512, HX), f32),
        ((OUT, HX), f32),
        ((512, CELLS), f32),
        ((512, CELLS), bf16),
        ((512, CELLS), bf16),
        ((4 * 512, HX), f32),
        ((TZ * TY * 24, HX), f32),
        ((OUT, HX), f32),
        ((OUT, HX), f32),
        ((32, HX), f32),
    ]
    return pl.pallas_call(
        compute_kernel,
        out_shape=[jax.ShapeDtypeStruct(s, d) for s, d in shapes],
        in_specs=[VMEM] * 11,
        out_specs=[VMEM] * 7,
        scratch_shapes=[pltpu.VMEM(s, d) for s, d in scratch],
        compiler_params=pltpu.CompilerParams(vmem_limit_bytes=60 * 2**20),
        name="compute",
    )(
        fields, *halo, target.reshape(OUT * 64, HX), conv_w, conv_b.reshape(1, HID),
        down_w, down_b.reshape(1, OUT),
    )


def neighbour(dz, dy):
    nz, ny = lax.axis_size("gz"), lax.axis_size("gy")
    gz, gy = lax.axis_index("gz"), lax.axis_index("gy")
    return (lax.rem(gz + dz + nz, nz), lax.rem(gy + dy + ny, ny))


RIM = [(-1, 0), (1, 0), (0, -1), (0, 1), (-1, -1), (-1, 1), (1, -1), (1, 1)]


def greet(offsets):
    barrier = pltpu.get_barrier_semaphore()
    for dz, dy in offsets:
        pl.semaphore_signal(barrier, inc=1, device_id=neighbour(dz, dy), device_id_type=MESH)
    return lambda: pl.semaphore_wait(barrier, len(offsets))


def send(src, dst, sems, k, dz, dy):
    copy = pltpu.make_async_remote_copy(
        src_ref=src, dst_ref=dst, send_sem=sems.at[0, k], recv_sem=sems.at[1, k],
        device_id=neighbour(dz, dy), device_id_type=MESH,
    )
    copy.start()
    return copy


def halo_kernel(fields, zlo, zhi, ylo, yhi, corners, raw, ysend, csend, sems):
    wait = greet(RIM)
    for h in range(2):
        raw[h, 1536:2048, :] = jnp.zeros((512, HX), f32)
        for ch in range(C):
            for z in range(NZ):
                at = ch * 256 + z * NY
                raw[h, at : at + NY, :] = fields[ch, z, :, h * HX : (h + 1) * HX].astype(f32)
    for k, y in enumerate((0, NY - 1)):
        for h in range(2):
            ysend[k, :, h * HX : (h + 1) * HX] = raw[h, pl.ds(y, 48, stride=NY), :].astype(bf16)
    for k in range(4):
        at = (k // 2) * (NZ - 1) * NY + (k % 2) * (NY - 1)
        for h in range(2):
            csend[k, :, h * HX : (h + 1) * HX] = raw[h, pl.ds(at, 8, stride=256), :]
    wait()
    copies = [
        send(fields.at[:, NZ - 1], zlo, sems, 0, 1, 0),
        send(fields.at[:, 0], zhi, sems, 1, -1, 0),
        send(ysend.at[1], ylo, sems, 2, 0, 1),
        send(ysend.at[0], yhi, sems, 3, 0, -1),
    ]
    for k in range(4):
        dz, dy = 2 * (k // 2) - 1, 2 * (k % 2) - 1
        copies.append(send(csend.at[k], corners.at[3 - k], sems, 4 + k, dz, dy))
    for copy in copies:
        copy.wait()


def exchange_halo(fields):
    shapes = [
        ((C, NY, NX), bf16), ((C, NY, NX), bf16), ((C * NZ, NX), bf16), ((C * NZ, NX), bf16),
        ((4, 8, NX), f32),
    ]
    return pl.pallas_call(
        halo_kernel,
        out_shape=[jax.ShapeDtypeStruct(s, d) for s, d in shapes],
        in_specs=[VMEM],
        out_specs=[VMEM] * 5,
        scratch_shapes=[
            pltpu.VMEM((2, 2048, HX), f32),
            pltpu.VMEM((2, C * NZ, NX), bf16),
            pltpu.VMEM((4, 8, NX), f32),
            pltpu.SemaphoreType.DMA((2, 8)),
        ],
        compiler_params=pltpu.CompilerParams(collective_id=0, has_side_effects=True),
        name="halo",
    )(fields)


def reduce_kernel(
    nz, ny, sz, sy, sc, gd, gc, rz, ry, rc, gd_out, gc_out,
    gd_in, gc_in, gd_part, gc_part, gd_all, gc_all, gc_mine, sems,
):
    me_z, me_y = lax.axis_index("gz"), lax.axis_index("gy")
    peers = [(d, 0) for d in range(1, nz)] + [(0, d) for d in range(1, ny)]
    peers += [(dz, dy) for dz in (-1, 1) for dy in (-1, 1)]
    greet(peers)()
    first = []
    for d in range(1, nz):
        to = lax.rem(me_z + d, nz)
        rows = gd.at[pl.ds(pl.multiple_of(to * 8, 8), 8)]
        first.append(send(rows, gd_in.at[me_z], sems, d, d, 0))
    for d in range(1, ny):
        to = lax.rem(me_y + d, ny)
        rows = gc.at[pl.ds(pl.multiple_of(to * 8, 8), 8)]
        first.append(send(rows, gc_in.at[me_y], sems, nz + d, 0, d))
    k = nz + ny
    rims = [
        send(sz.at[0], rz.at[1], sems, k, -1, 0),
        send(sz.at[1], rz.at[0], sems, k + 1, 1, 0),
        send(sy.at[0], ry.at[1], sems, k + 2, 0, -1),
        send(sy.at[1], ry.at[0], sems, k + 3, 0, 1),
    ]
    for j in range(4):
        dz, dy = 2 * (j // 2) - 1, 2 * (j % 2) - 1
        rims.append(send(sc.at[j], rc.at[3 - j], sems, k + 4 + j, dz, dy))
    k += 8
    gd_in[me_z] = gd[pl.ds(pl.multiple_of(me_z * 8, 8), 8), :]
    gc_in[me_y] = gc[pl.ds(pl.multiple_of(me_y * 8, 8), 8), :]
    for copy in first:
        copy.wait()

    def added(ref, n):
        total = ref[0]
        for j in range(1, n):
            total = total + ref[j]
        return total

    gd_part[...] = added(gd_in, nz)
    gc_part[...] = added(gc_in, ny)
    second = [send(gd_part, gd_all.at[me_y], sems, k + d, 0, d) for d in range(1, ny)]
    k += ny
    second += [send(gc_part, gc_all.at[me_z], sems, k + d, d, 0) for d in range(1, nz)]
    k += nz
    gd_all[me_y] = gd_part[...]
    gc_all[me_z] = gc_part[...]
    for copy in second:
        copy.wait()
    gd_out[...] = added(gd_all, ny)
    gc_mine[...] = added(gc_all, nz)
    third = [send(gc_mine, gc_out.at[me_y], sems, k + d, 0, d) for d in range(1, ny)]
    gc_out[me_y] = gc_mine[...]
    for copy in third + rims:
        copy.wait()


def reduce_all(sz, sy, sc, gd, gc):
    nz, ny = lax.axis_size("gz"), lax.axis_size("gy")
    shapes = [
        (sz.shape, bf16), (sy.shape, bf16), (sc.shape, f32), ((8, 512), f32), ((8, 8, 384), f32),
    ]
    scratch = [
        (nz, 8, 512), (ny, 8, 384), (8, 512), (8, 384), (ny, 8, 512), (nz, 8, 384), (8, 384),
    ]
    return pl.pallas_call(
        functools.partial(reduce_kernel, nz, ny),
        out_shape=[jax.ShapeDtypeStruct(s, d) for s, d in shapes],
        in_specs=[VMEM] * 5,
        out_specs=[VMEM] * 5,
        scratch_shapes=[pltpu.VMEM(s, f32) for s in scratch]
        + [pltpu.SemaphoreType.DMA((2, 2 * nz + 3 * ny + 8))],
        compiler_params=pltpu.CompilerParams(collective_id=1, has_side_effects=True),
        name="reduce",
    )(sz, sy, sc, gd, gc)


def finish_kernel(cells, sens, rz, ry, rc, gd, gc, sens_out, conv, cbias, down, dbias, loss):
    row = iota((NY, NX), 0)
    sides = [ry[0].astype(f32), ry[1].astype(f32)]
    for ch in range(C):
        for z in range(NZ):
            i = ch * NZ + z
            value = sens[i * NY : (i + 1) * NY, :]
            low, high = sides[0][i : i + 1], sides[1][i : i + 1]
            if z in (0, NZ - 1):
                side = 0 if z == 0 else 1
                value = value + rz[side, ch * NY : (ch + 1) * NY, :].astype(f32)
                low = low + rc[2 * side, ch : ch + 1, :]
                high = high + rc[2 * side + 1, ch : ch + 1, :]
            value = value + jnp.where(row == 0, low, 0.0)
            value = value + jnp.where(row == NY - 1, high, 0.0)
            sens_out[i * NY : (i + 1) * NY, :] = value
    total = gc[...].reshape(HID, 384)
    exact = functools.partial(
        lax.dot_general, dimension_numbers=NT, preferred_element_type=f32,
        precision=lax.Precision.HIGHEST,
    )
    scale = 1.0 / cells
    conv[...] = exact(total, tap_matrix(384)) * scale
    lane, r = iota((8, 384), 1), iota((8, 384), 0)
    pick = one_hot(lane == jnp.where(r == 0, 24, r + 27))
    rows = exact(pick, total) * scale
    cbias[...] = rows[0:1]
    dbias[...] = rows[1:3]
    down[...] = gd[...] * scale
    square = jnp.where(iota((HID, 384), 1) == 30, total, 0.0)
    loss[...] = jnp.sum(square, keepdims=True) * (scale / OUT)


def finish(sens, rz, ry, rc, gd, gc):
    cells = 64 * HX * lax.axis_size("gz") * lax.axis_size("gy")
    shapes = [sens.shape, (HID, C * 27), (1, HID), (8, 512), (2, HID), (1, 1)]
    return pl.pallas_call(
        functools.partial(finish_kernel, cells),
        out_shape=[jax.ShapeDtypeStruct(s, f32) for s in shapes],
        in_specs=[VMEM] * 6,
        out_specs=[VMEM] * 6,
        name="finish",
    )(sens, rz, ry, rc, gd, gc)


def on_device(fields, target, conv_w, conv_b, down_w, down_b):
    halo = exchange_halo(fields)
    out, sens, sz, sy, sc, gd, gc = compute(fields, halo, target, conv_w, conv_b, down_w, down_b)
    rz, ry, rc, gd, gc = reduce_all(sz, sy, sc, gd, gc)
    sens, conv, cbias, down, dbias, loss = finish(sens, rz, ry, rc, gd, gc)
    return (
        out.reshape(target.shape),
        sens.reshape(fields.shape),
        conv,
        cbias.reshape(HID),
        down,
        dbias.reshape(OUT),
        loss.reshape(()),
    )


def solution(mesh):
    block = P(None, "gz", "gy", None)
    return jax.shard_map(
        on_device,
        mesh=mesh,
        in_specs=(block, block, P(), P(), P(), P()),
        out_specs=(block, block, P(), P(), P("gz", None), P(), P()),
        check_vma=False,
    )
```

```python
import functools
import jax
import jax.numpy as jnp
from jax import lax
from jax.experimental import pallas as pl
from jax.experimental.pallas import tpu as pltpu
from jax.sharding import PartitionSpec as P

f32, bf16 = jnp.float32, jnp.bfloat16
MESH = pl.DeviceIdType.MESH
C, NZ, NY, NX = 6, 8, 32, 256
HID, OUT = 64, 128
TZ, TY = NZ + 2, NY + 2
HX = NX // 2
ROWS = 4
CELLS = ROWS * HX
SCALE = 0.7978845608028654
CUBIC = 0.044715
NT = (((1,), (1,)), ((), ()))
FLAGS = {}
VMEM = pl.BlockSpec(memory_space=pltpu.VMEM)


def dot(a, b):
    return jnp.dot(a, b, preferred_element_type=f32)


def dot_nt(a, b):
    return lax.dot_general(a, b, NT, preferred_element_type=f32)


def iota(shape, dim):
    return lax.broadcasted_iota(jnp.int32, shape, dim)


def one_hot(mask):
    return jnp.where(mask, 1.0, 0.0)


def split_matrix():
    lane = iota((NX, 4 * HX), 1)
    want = lax.rem(2 * lax.rem(lane, HX) + lane // HX - 1 + NX, NX)
    return one_hot(iota((NX, 4 * HX), 0) == want).astype(bf16)


def tap_matrix(cols):
    lane = iota((C * 27, cols), 1)
    a, b = lane // 128, lax.rem(lane // 32, 4)
    ch, c = lax.rem(lane // 4, 8), lax.rem(lane, 4)
    ok = (a < 3) & (b < 3) & (c < 3) & (ch < C)
    want = jnp.where(ok, ch * 27 + 9 * a + 3 * b + c, -1)
    return one_hot(iota((C * 27, cols), 0) == want)


def column(row, n):
    eye = iota((n, n), 0) == iota((n, n), 1)
    return jnp.sum(jnp.where(eye, jnp.broadcast_to(row, (n, n)), 0.0), axis=1, keepdims=True)


def halves(x):
    hi = x.astype(bf16)
    return hi, (x - hi.astype(f32)).astype(bf16)


def row_swap():
    r, k = iota((256, 256), 0), iota((256, 256), 1)
    return one_hot(k == lax.rem(r, 16) * 16 + r // 16).astype(bf16)


def tile_order(count, blocks, ones_at):
    r, k = iota((count * 32, ones_at + 8), 0), iota((count * 32, ones_at + 8), 1)
    block = lax.rem(r, 32)
    return one_hot(k == jnp.where(block < blocks, block * count + r // 32, ones_at)).astype(bf16)


def compute_kernel(
    fields, zlo, zhi, ylo, yhi, corners, target, conv_w, conv_b, down_w, down_b,
    out_ref, sens, sz, sy, sc, gd, gc_out,
    split, order, swap, tiles, tgt, outs, wb, wbt, wdt, wd, wtmp, db,
    pre_a, pre_b, hid_a, hid_b, slope_a, slope_b, gp, gc, acc, dsum, sqsum, ytmp,
):
    split[...] = split_matrix()
    order[...] = tile_order(8, 24, 192)
    swap[...] = row_swap()

    def tiles_of(parts, count, starts):
        cols = []
        for g in range(count // 8):
            rows = [
                parts[ch * count + g * 8 : ch * count + g * 8 + 8, dx * HX : (dx + 1) * HX]
                for ch in range(C)
                for dx in range(4)
            ]
            cols.append(jnp.concatenate(rows + [jnp.ones((8, HX), f32)], axis=0))
        return dot(order[...], jnp.concatenate(cols, axis=1).astype(bf16)).astype(bf16)

    def put_plane(value, at):
        done = tiles_of(dot(value, split[...]), NY, 4)
        for g in range(4):
            rows = pl.ds(pl.multiple_of(at + g * 256, 32), 256)
            tiles[rows, :] = done[:, g * HX : (g + 1) * HX]

    def plane(z, carry):
        put_plane(fields[:, z].reshape(C * NY, NX), ((z + 1) * TY + 1) * 32)
        return carry

    lax.fori_loop(0, NZ, plane, 0)
    put_plane(zlo[...].reshape(C * NY, NX), 32)
    put_plane(zhi[...].reshape(C * NY, NX), ((NZ + 1) * TY + 1) * 32)
    for side, value in ((0, ylo), (NY + 1, yhi)):
        done = tiles_of(dot(value[...], split[...]), NZ, 1)
        for z in range(NZ):
            at = ((z + 1) * TY + side) * 32
            tiles[at : at + 32, :] = done[z * 32 : z * 32 + 32, :]
    cols = []
    for k in range(4):
        parts = dot(corners[k].astype(bf16), split[...])
        rows = [parts[:, dx * HX : (dx + 1) * HX] for dx in range(4)]
        cols.append(jnp.concatenate(rows + [jnp.ones((8, HX), f32)], axis=0))
    r, k = iota((32, 40), 0), iota((32, 40), 1)
    small = one_hot(k == jnp.where(r < 24, lax.rem(r, 4) * 8 + r // 4, 32)).astype(bf16)
    done = dot(small, jnp.concatenate(cols, axis=1).astype(bf16)).astype(bf16)
    for k in range(4):
        tile = (k // 2) * (NZ + 1) * TY + (k % 2) * (NY + 1)
        tiles[tile * 32 : tile * 32 + 32, :] = done[:, k * HX : (k + 1) * HX]

    def swapped(pieces):
        halves_ = [jnp.concatenate(p, axis=0) for p in pieces]
        return dot(swap[...], jnp.concatenate(halves_, axis=1)).astype(bf16)

    def turn_target(z, carry):
        for pair in range(4):
            pieces = []
            for half in range(2):
                first = (pair * 2 + half) * 16
                pieces.append([
                    target[pl.ds(pl.multiple_of((first + o) * 64 + z * 16, 16), 16), :]
                    for o in range(16)
                ])
            done = swapped(pieces)
            for half in range(2):
                first = (pair * 2 + half) * 16
                for y in range(16):
                    at = pl.ds(pl.multiple_of((z * 16 + y) * OUT + first, 16), 16)
                    tgt[at, :] = done[y * 16 : y * 16 + 16, half * HX : (half + 1) * HX]
        return carry

    lax.fori_loop(0, 4, turn_target, 0)

    taps = tap_matrix(512).astype(bf16)
    base = dot(conv_w[...], taps)
    bias = column(conv_b[...], HID)
    b_hi = bias.astype(bf16).astype(f32)
    b_mid = (bias - b_hi).astype(bf16).astype(f32)
    b_lo = bias - b_hi - b_mid
    lane = iota((HID, 512), 1)
    for par in range(8):
        shift = (par // 4) * 128 + (par // 2 % 2) * 32 + par % 2
        moved = pltpu.roll(base, shift, 1) if shift else base
        moved = jnp.where(lane == 24, b_hi, moved)
        moved = jnp.where(lane == 25, b_mid, moved)
        moved = jnp.where(lane == 26, b_lo, moved)
        for q in range(4):
            wtmp[q, pl.ds(par, HID, stride=8), :] = moved[:, q * 128 : (q + 1) * 128]
    for q in range(4):
        wb[:, q * 128 : (q + 1) * 128] = wtmp[q].astype(bf16)
    row = iota((384, 512), 0)
    keep = one_hot(iota((384, 512), 1) == (row // 24) * 32 + lax.rem(row, 24)).astype(bf16)
    wbt[...] = dot_nt(keep, wb[...]).astype(bf16)
    wd[...] = (down_w[...].astype(f32) * 0.5).astype(bf16)
    eye = one_hot(iota((512, 512), 0) == iota((512, 512), 1)).astype(bf16)
    wdt[...] = dot_nt(eye, wd[...]).astype(bf16)
    db[...] = jnp.broadcast_to(column(down_b[...], OUT), (OUT, HX))

    gd[...] = jnp.zeros_like(gd)
    gc[...] = jnp.zeros_like(gc)
    dsum[...] = jnp.zeros_like(dsum)
    sqsum[...] = jnp.zeros_like(sqsum)

    def clear(i, carry):
        acc[pl.ds(pl.multiple_of(i * 240, 8), 240), :] = jnp.zeros((240, HX), f32)
        return carry

    lax.fori_loop(0, TZ * TY // 10, clear, 0)

    per = 16 // ROWS

    def window(i):
        zc, y0 = i // per, lax.rem(i, per) * ROWS
        cols = []
        for r in range(ROWS):
            parts = []
            for dz in range(4):
                at = ((2 * zc + dz) * TY + 2 * (y0 + r)) * 32
                parts.append(tiles[pl.ds(pl.multiple_of(at, 64), 128), :])
            cols.append(jnp.concatenate(parts, axis=0))
        return jnp.concatenate(cols, axis=1)

    def matmul(i, pre):
        pre[...] = dot(wb[...], window(i))

    def gelu(pre, hid, slope):
        for m in range(0, 512, 16):
            x = pre[m : m + 16, :]
            x2 = x * x
            t = jnp.tanh(x * (x2 * (SCALE * CUBIC) + SCALE))
            v = 1.0 + t
            h = x * v
            hid[m : m + 16, :] = h.astype(bf16)
            slope[m : m + 16, :] = v + (h * (1.0 - t)) * (x2 * (3 * SCALE * CUBIC) + SCALE)

    def backward(i, hid, slope):
        zc, y0 = i // per, lax.rem(i, per) * ROWS
        output = dot(wd[...], hid[...])
        go, ds, sq = [], 0.0, 0.0
        for r in range(ROWS):
            at = pl.ds(pl.multiple_of((zc * 16 + y0 + r) * OUT, OUT), OUT)
            value = output[:, r * HX : (r + 1) * HX] + db[...]
            outs[at, :] = value.astype(bf16)
            diff = value - tgt[at, :].astype(f32)
            ds = ds + diff
            sq = sq + diff * diff
            go.append(diff.astype(bf16))
        dsum[...] += ds
        sqsum[...] += sq
        go = jnp.concatenate(go, axis=1)
        gd[...] += dot_nt(go, hid[...])
        back = dot(wdt[...], go)
        gp[...] = (back * slope[...]).astype(bf16)
        grad = dot_nt(gp[...], window(i))
        for q in range(4):
            gc[q * 512 : (q + 1) * 512, :] += grad[:, q * 128 : (q + 1) * 128]
        spread = dot(wbt[...], gp[...])
        for dz in range(4):
            for k in range(2 * ROWS + 2):
                total = None
                for r in range(ROWS):
                    dy = k - 2 * r
                    if 0 <= dy < 4:
                        m = (dz * 4 + dy) * 24
                        piece = spread[m : m + 24, r * HX : (r + 1) * HX]
                        total = piece if total is None else total + piece
                at = ((2 * zc + dz) * TY + 2 * y0 + k) * 24
                at = pl.ds(pl.multiple_of(at, 8), 24)
                acc[at, :] += total

    n = 64 // ROWS
    matmul(0, pre_a)
    gelu(pre_a, hid_a, slope_a)
    matmul(1, pre_b)

    def pair(j, carry):
        backward(2 * j, hid_a, slope_a)
        matmul(2 * j + 2, pre_a)
        gelu(pre_b, hid_b, slope_b)
        backward(2 * j + 1, hid_b, slope_b)
        matmul(2 * j + 3, pre_b)
        gelu(pre_a, hid_a, slope_a)
        return carry

    lax.fori_loop(0, n // 2 - 1, pair, 0)
    backward(n - 2, hid_a, slope_a)
    gelu(pre_b, hid_b, slope_b)
    backward(n - 1, hid_b, slope_b)
    gd[...] = gd[...] * 0.5

    def turn_out(z, carry):
        for pair_ in range(4):
            pieces = []
            for half in range(2):
                first = (pair_ * 2 + half) * 16
                pieces.append([
                    outs[pl.ds(pl.multiple_of((z * 16 + y) * OUT + first, 16), 16), :]
                    for y in range(16)
                ])
            done = swapped(pieces)
            for half in range(2):
                first = (pair_ * 2 + half) * 16
                for o in range(16):
                    at = pl.ds(pl.multiple_of((first + o) * 64 + z * 16, 16), 16)
                    out_ref[at, :] = done[o * 16 : o * 16 + 16, half * HX : (half + 1) * HX]
        return carry

    lax.fori_loop(0, 4, turn_out, 0)

    def join(rows):
        hi, lo = halves(jnp.concatenate(rows, axis=1))
        return dot_nt(hi, split[...]) + dot_nt(lo, split[...])

    def gather(start, count, stride):
        parts = []
        for dx in range(4):
            pieces = [acc[pl.ds(start + ch * 4 + dx, count, stride=stride), :] for ch in range(C)]
            parts.append(jnp.concatenate(pieces, axis=0))
        return join(parts)

    def sens_plane(z, carry):
        value = gather(((z + 1) * TY + 1) * 24, NY, 24)
        for ch in range(C):
            at = pl.multiple_of(ch * NZ * NY + z * NY, NY)
            sens[pl.ds(at, NY), :] = value[ch * NY : (ch + 1) * NY]
        return carry

    lax.fori_loop(0, NZ, sens_plane, 0)
    sz[0] = gather(24, NY, 24).astype(bf16)
    sz[1] = gather(((NZ + 1) * TY + 1) * 24, NY, 24).astype(bf16)
    sy[0] = gather(TY * 24, NZ, TY * 24).astype(bf16)
    sy[1] = gather((TY + NY + 1) * 24, NZ, TY * 24).astype(bf16)
    ytmp[...] = jnp.zeros_like(ytmp)
    for k in range(4):
        tile = (k // 2) * (NZ + 1) * TY + (k % 2) * (NY + 1)
        ytmp[0:24, :] = acc[tile * 24 : tile * 24 + 24, :]
        sc[k] = join([ytmp[pl.ds(dx, 8, stride=4), :] for dx in range(4)])

    total = None
    for par in range(8):
        shift = (par // 4) * 128 + (par // 2 % 2) * 32 + par % 2
        part = jnp.concatenate(
            [gc[pl.ds(q * 512 + par, HID, stride=8), :] for q in range(4)], axis=1
        )
        part = pltpu.roll(part, 512 - shift, 1) if shift else part
        total = part if total is None else total + part
    total = total[:, :384]
    lane = iota((HID, 384), 1)
    dcol = jnp.sum(dsum[...], axis=1, keepdims=True)
    scol = jnp.sum(sqsum[...], axis=1, keepdims=True)
    total = jnp.where(lane == 28, dcol[:HID], total)
    total = jnp.where(lane == 29, dcol[HID:], total)
    total = jnp.where(lane == 30, scol[:HID] + scol[HID:], total)
    gc_out[...] = total


def compute(fields, halo, target, conv_w, conv_b, down_w, down_b):
    shapes = [
        ((OUT * 64, HX), bf16),
        ((C * NZ * NY, NX), f32),
        ((2, C * NY, NX), bf16),
        ((2, C * NZ, NX), bf16),
        ((4, 8, NX), f32),
        ((OUT, 512), f32),
        ((HID, 384), f32),
    ]
    scratch = [
        ((NX, 4 * HX), bf16),
        ((256, 200), bf16),
        ((256, 256), bf16),
        ((TZ * TY * 32, HX), bf16),
        ((OUT * 64, HX), bf16),
        ((OUT * 64, HX), bf16),
        ((512, 512), bf16),
        ((384, 512), bf16),
        ((512, OUT), bf16),
        ((OUT, 512), bf16),
        ((4, 512, HX), f32),
        ((OUT, HX), f32),
        ((512, CELLS), f32),
        ((512, CELLS), f32),
        ((512, CELLS), bf16),
        ((512, CELLS), bf16),
        ((512, CELLS), f32),
        ((512, CELLS), f32),
        ((512, CELLS), bf16),
        ((4 * 512, HX), f32),
        ((TZ * TY * 24, HX), f32),
        ((OUT, HX), f32),
        ((OUT, HX), f32),
        ((32, HX), f32),
    ]
    return pl.pallas_call(
        compute_kernel,
        out_shape=[jax.ShapeDtypeStruct(s, d) for s, d in shapes],
        in_specs=[VMEM] * 11,
        out_specs=[VMEM] * 7,
        scratch_shapes=[pltpu.VMEM(s, d) for s, d in scratch],
        compiler_params=pltpu.CompilerParams(vmem_limit_bytes=60 * 2**20, flags=FLAGS),
        name="compute",
    )(
        fields, *halo, target.reshape(OUT * 64, HX), conv_w, conv_b.reshape(1, HID),
        down_w, down_b.reshape(1, OUT),
    )


def neighbour(dz, dy):
    nz, ny = lax.axis_size("gz"), lax.axis_size("gy")
    gz, gy = lax.axis_index("gz"), lax.axis_index("gy")
    return (lax.rem(gz + dz + nz, nz), lax.rem(gy + dy + ny, ny))


RIM = [(-1, 0), (1, 0), (0, -1), (0, 1), (-1, -1), (-1, 1), (1, -1), (1, 1)]


def greet(offsets):
    barrier = pltpu.get_barrier_semaphore()
    for dz, dy in offsets:
        pl.semaphore_signal(barrier, inc=1, device_id=neighbour(dz, dy), device_id_type=MESH)
    return lambda: pl.semaphore_wait(barrier, len(offsets))


def send(src, dst, sems, k, dz, dy):
    copy = pltpu.make_async_remote_copy(
        src_ref=src, dst_ref=dst, send_sem=sems.at[0, k], recv_sem=sems.at[1, k],
        device_id=neighbour(dz, dy), device_id_type=MESH,
    )
    copy.start()
    return copy


def halo_kernel(fields, zlo, zhi, ylo, yhi, corners, raw, ysend, csend, sems):
    wait = greet(RIM)
    for h in range(2):
        raw[h, 1536:2048, :] = jnp.zeros((512, HX), f32)
        for ch in range(C):
            for z in range(NZ):
                at = ch * 256 + z * NY
                raw[h, at : at + NY, :] = fields[ch, z, :, h * HX : (h + 1) * HX].astype(f32)
    for k, y in enumerate((0, NY - 1)):
        for h in range(2):
            ysend[k, :, h * HX : (h + 1) * HX] = raw[h, pl.ds(y, 48, stride=NY), :].astype(bf16)
    for k in range(4):
        at = (k // 2) * (NZ - 1) * NY + (k % 2) * (NY - 1)
        for h in range(2):
            csend[k, :, h * HX : (h + 1) * HX] = raw[h, pl.ds(at, 8, stride=256), :]
    wait()
    copies = [
        send(fields.at[:, NZ - 1], zlo, sems, 0, 1, 0),
        send(fields.at[:, 0], zhi, sems, 1, -1, 0),
        send(ysend.at[1], ylo, sems, 2, 0, 1),
        send(ysend.at[0], yhi, sems, 3, 0, -1),
    ]
    for k in range(4):
        dz, dy = 2 * (k // 2) - 1, 2 * (k % 2) - 1
        copies.append(send(csend.at[k], corners.at[3 - k], sems, 4 + k, dz, dy))
    for copy in copies:
        copy.wait()


def exchange_halo(fields):
    shapes = [
        ((C, NY, NX), bf16), ((C, NY, NX), bf16), ((C * NZ, NX), bf16), ((C * NZ, NX), bf16),
        ((4, 8, NX), f32),
    ]
    return pl.pallas_call(
        halo_kernel,
        out_shape=[jax.ShapeDtypeStruct(s, d) for s, d in shapes],
        in_specs=[VMEM],
        out_specs=[VMEM] * 5,
        scratch_shapes=[
            pltpu.VMEM((2, 2048, HX), f32),
            pltpu.VMEM((2, C * NZ, NX), bf16),
            pltpu.VMEM((4, 8, NX), f32),
            pltpu.SemaphoreType.DMA((2, 8)),
        ],
        compiler_params=pltpu.CompilerParams(collective_id=0, has_side_effects=True),
        name="halo",
    )(fields)


def reduce_kernel(
    nz, ny, sz, sy, sc, gd, gc, rz, ry, rc, gd_out, gc_out,
    gd_in, gc_in, gd_part, gc_part, gd_all, gc_all, gc_mine, sems,
):
    me_z, me_y = lax.axis_index("gz"), lax.axis_index("gy")
    peers = [(d, 0) for d in range(1, nz)] + [(0, d) for d in range(1, ny)]
    peers += [(dz, dy) for dz in (-1, 1) for dy in (-1, 1)]
    greet(peers)()
    first = []
    for d in range(1, nz):
        to = lax.rem(me_z + d, nz)
        rows = gd.at[pl.ds(pl.multiple_of(to * 8, 8), 8)]
        first.append(send(rows, gd_in.at[me_z], sems, d, d, 0))
    for d in range(1, ny):
        to = lax.rem(me_y + d, ny)
        rows = gc.at[pl.ds(pl.multiple_of(to * 8, 8), 8)]
        first.append(send(rows, gc_in.at[me_y], sems, nz + d, 0, d))
    k = nz + ny
    rims = [
        send(sz.at[0], rz.at[1], sems, k, -1, 0),
        send(sz.at[1], rz.at[0], sems, k + 1, 1, 0),
        send(sy.at[0], ry.at[1], sems, k + 2, 0, -1),
        send(sy.at[1], ry.at[0], sems, k + 3, 0, 1),
    ]
    for j in range(4):
        dz, dy = 2 * (j // 2) - 1, 2 * (j % 2) - 1
        rims.append(send(sc.at[j], rc.at[3 - j], sems, k + 4 + j, dz, dy))
    k += 8
    gd_in[me_z] = gd[pl.ds(pl.multiple_of(me_z * 8, 8), 8), :]
    gc_in[me_y] = gc[pl.ds(pl.multiple_of(me_y * 8, 8), 8), :]
    for copy in first:
        copy.wait()

    def added(ref, n):
        total = ref[0]
        for j in range(1, n):
            total = total + ref[j]
        return total

    gd_part[...] = added(gd_in, nz)
    gc_part[...] = added(gc_in, ny)
    second = [send(gd_part, gd_all.at[me_y], sems, k + d, 0, d) for d in range(1, ny)]
    k += ny
    second += [send(gc_part, gc_all.at[me_z], sems, k + d, d, 0) for d in range(1, nz)]
    k += nz
    gd_all[me_y] = gd_part[...]
    gc_all[me_z] = gc_part[...]
    for copy in second:
        copy.wait()
    gd_out[...] = added(gd_all, ny)
    gc_mine[...] = added(gc_all, nz)
    third = [send(gc_mine, gc_out.at[me_y], sems, k + d, 0, d) for d in range(1, ny)]
    gc_out[me_y] = gc_mine[...]
    for copy in third + rims:
        copy.wait()


def reduce_all(sz, sy, sc, gd, gc):
    nz, ny = lax.axis_size("gz"), lax.axis_size("gy")
    shapes = [
        (sz.shape, bf16), (sy.shape, bf16), (sc.shape, f32), ((8, 512), f32), ((8, 8, 384), f32),
    ]
    scratch = [
        (nz, 8, 512), (ny, 8, 384), (8, 512), (8, 384), (ny, 8, 512), (nz, 8, 384), (8, 384),
    ]
    return pl.pallas_call(
        functools.partial(reduce_kernel, nz, ny),
        out_shape=[jax.ShapeDtypeStruct(s, d) for s, d in shapes],
        in_specs=[VMEM] * 5,
        out_specs=[VMEM] * 5,
        scratch_shapes=[pltpu.VMEM(s, f32) for s in scratch]
        + [pltpu.SemaphoreType.DMA((2, 2 * nz + 3 * ny + 8))],
        compiler_params=pltpu.CompilerParams(collective_id=1, has_side_effects=True),
        name="reduce",
    )(sz, sy, sc, gd, gc)


def finish_kernel(cells, sens, rz, ry, rc, gd, gc, sens_out, conv, cbias, down, dbias, loss):
    row = iota((NY, NX), 0)
    sides = [ry[0].astype(f32), ry[1].astype(f32)]
    for ch in range(C):
        for z in range(NZ):
            i = ch * NZ + z
            value = sens[i * NY : (i + 1) * NY, :]
            low, high = sides[0][i : i + 1], sides[1][i : i + 1]
            if z in (0, NZ - 1):
                side = 0 if z == 0 else 1
                value = value + rz[side, ch * NY : (ch + 1) * NY, :].astype(f32)
                low = low + rc[2 * side, ch : ch + 1, :]
                high = high + rc[2 * side + 1, ch : ch + 1, :]
            value = value + jnp.where(row == 0, low, 0.0)
            value = value + jnp.where(row == NY - 1, high, 0.0)
            sens_out[i * NY : (i + 1) * NY, :] = value
    total = gc[...].reshape(HID, 384)
    exact = functools.partial(
        lax.dot_general, dimension_numbers=NT, preferred_element_type=f32,
        precision=lax.Precision.HIGHEST,
    )
    scale = 1.0 / cells
    conv[...] = exact(total, tap_matrix(384)) * scale
    lane, r = iota((8, 384), 1), iota((8, 384), 0)
    pick = one_hot(lane == jnp.where(r == 0, 24, r + 27))
    rows = exact(pick, total) * scale
    cbias[...] = rows[0:1]
    dbias[...] = rows[1:3]
    down[...] = gd[...] * scale
    square = jnp.where(iota((HID, 384), 1) == 30, total, 0.0)
    loss[...] = jnp.sum(square, keepdims=True) * (scale / OUT)


def finish(sens, rz, ry, rc, gd, gc):
    cells = 64 * HX * lax.axis_size("gz") * lax.axis_size("gy")
    shapes = [sens.shape, (HID, C * 27), (1, HID), (8, 512), (2, HID), (1, 1)]
    return pl.pallas_call(
        functools.partial(finish_kernel, cells),
        out_shape=[jax.ShapeDtypeStruct(s, f32) for s in shapes],
        in_specs=[VMEM] * 6,
        out_specs=[VMEM] * 6,
        name="finish",
    )(sens, rz, ry, rc, gd, gc)


def on_device(fields, target, conv_w, conv_b, down_w, down_b):
    halo = exchange_halo(fields)
    out, sens, sz, sy, sc, gd, gc = compute(fields, halo, target, conv_w, conv_b, down_w, down_b)
    rz, ry, rc, gd, gc = reduce_all(sz, sy, sc, gd, gc)
    sens, conv, cbias, down, dbias, loss = finish(sens, rz, ry, rc, gd, gc)
    return (
        out.reshape(target.shape),
        sens.reshape(fields.shape),
        conv,
        cbias.reshape(HID),
        down,
        dbias.reshape(OUT),
        loss.reshape(()),
    )


def solution(mesh):
    block = P(None, "gz", "gy", None)
    return jax.shard_map(
        on_device,
        mesh=mesh,
        in_specs=(block, block, P(), P(), P(), P()),
        out_specs=(block, block, P(), P(), P("gz", None), P(), P()),
        check_vma=False,
    )
```

```python
import functools
import jax
import jax.numpy as jnp
from jax import lax
from jax.experimental import pallas as pl
from jax.experimental.pallas import tpu as pltpu
from jax.sharding import PartitionSpec as P

f32, bf16 = jnp.float32, jnp.bfloat16
MESH = pl.DeviceIdType.MESH
C, NZ, NY, NX = 6, 8, 32, 256
HID, OUT = 64, 128
TZ, TY = NZ + 2, NY + 2
HX = NX // 2
ROWS = 4
CELLS = ROWS * HX
SCALE = 0.7978845608028654
CUBIC = 0.044715
NT = (((1,), (1,)), ((), ()))
VMEM = pl.BlockSpec(memory_space=pltpu.VMEM)


def dot(a, b):
    return jnp.dot(a, b, preferred_element_type=f32)


def dot_nt(a, b):
    return lax.dot_general(a, b, NT, preferred_element_type=f32)


def iota(shape, dim):
    return lax.broadcasted_iota(jnp.int32, shape, dim)


def one_hot(mask):
    return jnp.where(mask, 1.0, 0.0)


def split_matrix():
    lane = iota((NX, 4 * HX), 1)
    want = lax.rem(2 * lax.rem(lane, HX) + lane // HX - 1 + NX, NX)
    return one_hot(iota((NX, 4 * HX), 0) == want).astype(bf16)


def tap_matrix(cols):
    lane = iota((C * 27, cols), 1)
    a, b = lane // 128, lax.rem(lane // 32, 4)
    ch, c = lax.rem(lane // 4, 8), lax.rem(lane, 4)
    ok = (a < 3) & (b < 3) & (c < 3) & (ch < C)
    want = jnp.where(ok, ch * 27 + 9 * a + 3 * b + c, -1)
    return one_hot(iota((C * 27, cols), 0) == want)


def column(row, n):
    eye = iota((n, n), 0) == iota((n, n), 1)
    return jnp.sum(jnp.where(eye, jnp.broadcast_to(row, (n, n)), 0.0), axis=1, keepdims=True)


def halves(x):
    hi = x.astype(bf16)
    return hi, (x - hi.astype(f32)).astype(bf16)


def neighbour(dz, dy):
    nz, ny = lax.axis_size("gz"), lax.axis_size("gy")
    gz, gy = lax.axis_index("gz"), lax.axis_index("gy")
    return (lax.rem(gz + dz + nz, nz), lax.rem(gy + dy + ny, ny))


def greet(offsets):
    barrier = pltpu.get_barrier_semaphore()
    for dz, dy in offsets:
        pl.semaphore_signal(barrier, inc=1, device_id=neighbour(dz, dy), device_id_type=MESH)
    return lambda: pl.semaphore_wait(barrier, len(offsets))


def send(src, dst, sems, k, dz, dy):
    copy = pltpu.make_async_remote_copy(
        src_ref=src, dst_ref=dst, send_sem=sems.at[0, k], recv_sem=sems.at[1, k],
        device_id=neighbour(dz, dy), device_id_type=MESH,
    )
    copy.start()
    return copy


def row_swap():
    r, k = iota((256, 256), 0), iota((256, 256), 1)
    return one_hot(k == lax.rem(r, 16) * 16 + r // 16).astype(bf16)


def tile_order(count, blocks, ones_at):
    r, k = iota((count * 32, ones_at + 8), 0), iota((count * 32, ones_at + 8), 1)
    block = lax.rem(r, 32)
    return one_hot(k == jnp.where(block < blocks, block * count + r // 32, ones_at)).astype(bf16)


def compute_kernel(
    nz, ny,
    fields, target, conv_w, conv_b, down_w, down_b,
    out_ref, sens, rz, ry, rc, gd_out, gc_out,
    zlo, zhi, ylo, yhi, corners, raw, ysend, csend, sz, sy, sc, gd, gc_sum,
    gd_in, gc_in, gd_part, gc_part, gd_all, gc_all, gc_mine,
    split, order, swap, tiles, tgt, outs, wb, wbt, wdt, wd, wtmp, db,
    pre_a, pre_b, hid_a, hid_b, slope_a, slope_b, gp, gc, acc, dsum, sqsum, ytmp, sems,
):
    me_z, me_y = lax.axis_index("gz"), lax.axis_index("gy")
    peers = [(d, 0) for d in range(1, nz)] + [(0, d) for d in range(1, ny)]
    peers += [(dz, dy) for dz in (-1, 1) for dy in (-1, 1)]
    entered = greet(peers)
    for h in range(2):
        raw[h, 1536:2048, :] = jnp.zeros((512, HX), f32)
        for ch in range(C):
            for z in range(NZ):
                at = ch * 256 + z * NY
                raw[h, at : at + NY, :] = fields[ch, z, :, h * HX : (h + 1) * HX].astype(f32)
    for k, y in enumerate((0, NY - 1)):
        for h in range(2):
            ysend[k, :, h * HX : (h + 1) * HX] = raw[h, pl.ds(y, 48, stride=NY), :].astype(bf16)
    for k in range(4):
        at = (k // 2) * (NZ - 1) * NY + (k % 2) * (NY - 1)
        for h in range(2):
            csend[k, :, h * HX : (h + 1) * HX] = raw[h, pl.ds(at, 8, stride=256), :]
    split[...] = split_matrix()
    order[...] = tile_order(8, 24, 192)
    swap[...] = row_swap()

    taps = tap_matrix(512).astype(bf16)
    base = dot(conv_w[...], taps)
    bias = column(conv_b[...], HID)
    b_hi = bias.astype(bf16).astype(f32)
    b_mid = (bias - b_hi).astype(bf16).astype(f32)
    b_lo = bias - b_hi - b_mid
    lane = iota((HID, 512), 1)
    for par in range(8):
        shift = (par // 4) * 128 + (par // 2 % 2) * 32 + par % 2
        moved = pltpu.roll(base, shift, 1) if shift else base
        moved = jnp.where(lane == 24, b_hi, moved)
        moved = jnp.where(lane == 25, b_mid, moved)
        moved = jnp.where(lane == 26, b_lo, moved)
        for q in range(4):
            wtmp[q, pl.ds(par, HID, stride=8), :] = moved[:, q * 128 : (q + 1) * 128]
    for q in range(4):
        wb[:, q * 128 : (q + 1) * 128] = wtmp[q].astype(bf16)
    row = iota((384, 512), 0)
    keep = one_hot(iota((384, 512), 1) == (row // 24) * 32 + lax.rem(row, 24)).astype(bf16)
    wbt[...] = dot_nt(keep, wb[...]).astype(bf16)
    wd[...] = (down_w[...].astype(f32) * 0.5).astype(bf16)
    eye = one_hot(iota((512, 512), 0) == iota((512, 512), 1)).astype(bf16)
    wdt[...] = dot_nt(eye, wd[...]).astype(bf16)
    db[...] = jnp.broadcast_to(column(down_b[...], OUT), (OUT, HX))

    entered()
    halo = [
        send(fields.at[:, NZ - 1], zlo, sems, 0, 1, 0),
        send(fields.at[:, 0], zhi, sems, 1, -1, 0),
        send(ysend.at[1], ylo, sems, 2, 0, 1),
        send(ysend.at[0], yhi, sems, 3, 0, -1),
    ]
    for k in range(4):
        dz, dy = 2 * (k // 2) - 1, 2 * (k % 2) - 1
        halo.append(send(csend.at[k], corners.at[3 - k], sems, 4 + k, dz, dy))

    def tiles_of(parts, count, starts):
        cols = []
        for g in range(count // 8):
            rows = [
                parts[ch * count + g * 8 : ch * count + g * 8 + 8, dx * HX : (dx + 1) * HX]
                for ch in range(C)
                for dx in range(4)
            ]
            cols.append(jnp.concatenate(rows + [jnp.ones((8, HX), f32)], axis=0))
        return dot(order[...], jnp.concatenate(cols, axis=1).astype(bf16)).astype(bf16)

    def put_plane(value, at):
        done = tiles_of(dot(value, split[...]), NY, 4)
        for g in range(4):
            rows = pl.ds(pl.multiple_of(at + g * 256, 32), 256)
            tiles[rows, :] = done[:, g * HX : (g + 1) * HX]

    def plane(z, carry):
        put_plane(fields[:, z].reshape(C * NY, NX), ((z + 1) * TY + 1) * 32)
        return carry

    lax.fori_loop(0, NZ, plane, 0)
    def swapped(pieces):
        halves_ = [jnp.concatenate(p, axis=0) for p in pieces]
        return dot(swap[...], jnp.concatenate(halves_, axis=1)).astype(bf16)

    def turn_target(z, carry):
        for pair in range(4):
            pieces = []
            for half in range(2):
                first = (pair * 2 + half) * 16
                pieces.append([
                    target[pl.ds(pl.multiple_of((first + o) * 64 + z * 16, 16), 16), :]
                    for o in range(16)
                ])
            done = swapped(pieces)
            for half in range(2):
                first = (pair * 2 + half) * 16
                for y in range(16):
                    at = pl.ds(pl.multiple_of((z * 16 + y) * OUT + first, 16), 16)
                    tgt[at, :] = done[y * 16 : y * 16 + 16, half * HX : (half + 1) * HX]
        return carry

    lax.fori_loop(0, 4, turn_target, 0)

    gd[...] = jnp.zeros_like(gd)
    gc[...] = jnp.zeros_like(gc)
    dsum[...] = jnp.zeros_like(dsum)
    sqsum[...] = jnp.zeros_like(sqsum)

    def clear(i, carry):
        acc[pl.ds(pl.multiple_of(i * 240, 8), 240), :] = jnp.zeros((240, HX), f32)
        return carry

    lax.fori_loop(0, TZ * TY // 10, clear, 0)

    for copy in halo:
        copy.wait()
    put_plane(zlo[...].reshape(C * NY, NX), 32)
    put_plane(zhi[...].reshape(C * NY, NX), ((NZ + 1) * TY + 1) * 32)
    for side, value in ((0, ylo), (NY + 1, yhi)):
        done = tiles_of(dot(value[...], split[...]), NZ, 1)
        for z in range(NZ):
            at = ((z + 1) * TY + side) * 32
            tiles[at : at + 32, :] = done[z * 32 : z * 32 + 32, :]
    cols = []
    for k in range(4):
        parts = dot(corners[k].astype(bf16), split[...])
        rows = [parts[:, dx * HX : (dx + 1) * HX] for dx in range(4)]
        cols.append(jnp.concatenate(rows + [jnp.ones((8, HX), f32)], axis=0))
    r, k = iota((32, 40), 0), iota((32, 40), 1)
    small = one_hot(k == jnp.where(r < 24, lax.rem(r, 4) * 8 + r // 4, 32)).astype(bf16)
    done = dot(small, jnp.concatenate(cols, axis=1).astype(bf16)).astype(bf16)
    for k in range(4):
        tile = (k // 2) * (NZ + 1) * TY + (k % 2) * (NY + 1)
        tiles[tile * 32 : tile * 32 + 32, :] = done[:, k * HX : (k + 1) * HX]

    per = 16 // ROWS

    def window(i):
        zc, y0 = i // per, lax.rem(i, per) * ROWS
        cols = []
        for r in range(ROWS):
            parts = []
            for dz in range(4):
                at = ((2 * zc + dz) * TY + 2 * (y0 + r)) * 32
                parts.append(tiles[pl.ds(pl.multiple_of(at, 64), 128), :])
            cols.append(jnp.concatenate(parts, axis=0))
        return jnp.concatenate(cols, axis=1)

    def matmul(i, pre):
        pre[...] = dot(wb[...], window(i))

    def gelu(pre, hid, slope):
        for m in range(0, 512, 16):
            x = pre[m : m + 16, :]
            x2 = x * x
            t = jnp.tanh(x * (x2 * (SCALE * CUBIC) + SCALE))
            v = 1.0 + t
            h = x * v
            hid[m : m + 16, :] = h.astype(bf16)
            slope[m : m + 16, :] = v + (h * (1.0 - t)) * (x2 * (3 * SCALE * CUBIC) + SCALE)

    def backward(i, hid, slope):
        zc, y0 = i // per, lax.rem(i, per) * ROWS
        output = dot(wd[...], hid[...])
        go, ds, sq = [], 0.0, 0.0
        for r in range(ROWS):
            at = pl.ds(pl.multiple_of((zc * 16 + y0 + r) * OUT, OUT), OUT)
            value = output[:, r * HX : (r + 1) * HX] + db[...]
            outs[at, :] = value.astype(bf16)
            diff = value - tgt[at, :].astype(f32)
            ds = ds + diff
            sq = sq + diff * diff
            go.append(diff.astype(bf16))
        dsum[...] += ds
        sqsum[...] += sq
        go = jnp.concatenate(go, axis=1)
        gd[...] += dot_nt(go, hid[...])
        back = dot(wdt[...], go)
        gp[...] = (back * slope[...]).astype(bf16)
        grad = dot_nt(gp[...], window(i))
        for q in range(4):
            gc[q * 512 : (q + 1) * 512, :] += grad[:, q * 128 : (q + 1) * 128]
        spread = dot(wbt[...], gp[...])
        for dz in range(4):
            for k in range(2 * ROWS + 2):
                total = None
                for r in range(ROWS):
                    dy = k - 2 * r
                    if 0 <= dy < 4:
                        m = (dz * 4 + dy) * 24
                        piece = spread[m : m + 24, r * HX : (r + 1) * HX]
                        total = piece if total is None else total + piece
                at = ((2 * zc + dz) * TY + 2 * y0 + k) * 24
                at = pl.ds(pl.multiple_of(at, 8), 24)
                acc[at, :] += total

    n = 64 // ROWS
    matmul(0, pre_a)
    gelu(pre_a, hid_a, slope_a)
    matmul(1, pre_b)

    def pair(j, carry):
        backward(2 * j, hid_a, slope_a)
        matmul(2 * j + 2, pre_a)
        gelu(pre_b, hid_b, slope_b)
        backward(2 * j + 1, hid_b, slope_b)
        matmul(2 * j + 3, pre_b)
        gelu(pre_a, hid_a, slope_a)
        return carry

    lax.fori_loop(0, n // 2 - 1, pair, 0)
    backward(n - 2, hid_a, slope_a)
    gelu(pre_b, hid_b, slope_b)
    backward(n - 1, hid_b, slope_b)
    gd[...] = gd[...] * 0.5


    total = None
    for par in range(8):
        shift = (par // 4) * 128 + (par // 2 % 2) * 32 + par % 2
        part = jnp.concatenate(
            [gc[pl.ds(q * 512 + par, HID, stride=8), :] for q in range(4)], axis=1
        )
        part = pltpu.roll(part, 512 - shift, 1) if shift else part
        total = part if total is None else total + part
    total = total[:, :384]
    lane = iota((HID, 384), 1)
    dcol = jnp.sum(dsum[...], axis=1, keepdims=True)
    scol = jnp.sum(sqsum[...], axis=1, keepdims=True)
    total = jnp.where(lane == 28, dcol[:HID], total)
    total = jnp.where(lane == 29, dcol[HID:], total)
    total = jnp.where(lane == 30, scol[:HID] + scol[HID:], total)
    gc_sum[...] = total
    gd_in[me_z] = gd[pl.ds(pl.multiple_of(me_z * 8, 8), 8), :]
    gc_in[me_y] = gc_sum[pl.ds(pl.multiple_of(me_y * 8, 8), 8), :]
    first = []
    k = 16
    for d in range(1, nz):
        to = lax.rem(me_z + d, nz)
        rows = gd.at[pl.ds(pl.multiple_of(to * 8, 8), 8)]
        first.append(send(rows, gd_in.at[me_z], sems, k + d, d, 0))
    for d in range(1, ny):
        to = lax.rem(me_y + d, ny)
        rows = gc_sum.at[pl.ds(pl.multiple_of(to * 8, 8), 8)]
        first.append(send(rows, gc_in.at[me_y], sems, k + nz + d, 0, d))

    def join(rows):
        hi, lo = halves(jnp.concatenate(rows, axis=1))
        return dot_nt(hi, split[...]) + dot_nt(lo, split[...])

    def gather(start, count, stride):
        parts = []
        for dx in range(4):
            pieces = [acc[pl.ds(start + ch * 4 + dx, count, stride=stride), :] for ch in range(C)]
            parts.append(jnp.concatenate(pieces, axis=0))
        return join(parts)

    sz[0] = gather(24, NY, 24).astype(bf16)
    sz[1] = gather(((NZ + 1) * TY + 1) * 24, NY, 24).astype(bf16)
    sy[0] = gather(TY * 24, NZ, TY * 24).astype(bf16)
    sy[1] = gather((TY + NY + 1) * 24, NZ, TY * 24).astype(bf16)
    ytmp[...] = jnp.zeros_like(ytmp)
    for k in range(4):
        tile = (k // 2) * (NZ + 1) * TY + (k % 2) * (NY + 1)
        ytmp[0:24, :] = acc[tile * 24 : tile * 24 + 24, :]
        sc[k] = join([ytmp[pl.ds(dx, 8, stride=4), :] for dx in range(4)])
    rims = [
        send(sz.at[0], rz.at[1], sems, 8, -1, 0),
        send(sz.at[1], rz.at[0], sems, 9, 1, 0),
        send(sy.at[0], ry.at[1], sems, 10, 0, -1),
        send(sy.at[1], ry.at[0], sems, 11, 0, 1),
    ]
    for j in range(4):
        dz, dy = 2 * (j // 2) - 1, 2 * (j % 2) - 1
        rims.append(send(sc.at[j], rc.at[3 - j], sems, 12 + j, dz, dy))

    def added(ref, n):
        total = ref[0]
        for j in range(1, n):
            total = total + ref[j]
        return total

    def sens_plane(z, carry):
        value = gather(((z + 1) * TY + 1) * 24, NY, 24)
        for ch in range(C):
            at = pl.multiple_of(ch * NZ * NY + z * NY, NY)
            sens[pl.ds(at, NY), :] = value[ch * NY : (ch + 1) * NY]
        return carry

    lax.fori_loop(0, NZ, sens_plane, 0)
    for copy in first:
        copy.wait()
    gc_part[...] = added(gc_in, ny)
    gd_part[...] = added(gd_in, nz)
    k = 16 + nz + ny
    second = [send(gc_part, gc_all.at[me_z], sems, k + d, d, 0) for d in range(1, nz)]
    k += nz
    second += [send(gd_part, gd_all.at[me_y], sems, k + d, 0, d) for d in range(1, ny)]
    k += ny
    gd_all[me_y] = gd_part[...]
    gc_all[me_z] = gc_part[...]
    def turn_out(z, carry):
        for pair_ in range(4):
            pieces = []
            for half in range(2):
                first = (pair_ * 2 + half) * 16
                pieces.append([
                    outs[pl.ds(pl.multiple_of((z * 16 + y) * OUT + first, 16), 16), :]
                    for y in range(16)
                ])
            done = swapped(pieces)
            for half in range(2):
                first = (pair_ * 2 + half) * 16
                for o in range(16):
                    at = pl.ds(pl.multiple_of((first + o) * 64 + z * 16, 16), 16)
                    out_ref[at, :] = done[o * 16 : o * 16 + 16, half * HX : (half + 1) * HX]
        return carry

    lax.fori_loop(0, 4, turn_out, 0)
    for copy in second:
        copy.wait()
    gc_mine[...] = added(gc_all, nz)
    third = [send(gc_mine, gc_out.at[me_y], sems, k + d, 0, d) for d in range(1, ny)]
    gc_out[me_y] = gc_mine[...]
    gd_out[...] = added(gd_all, ny)
    for copy in third + rims:
        copy.wait()


def compute(fields, target, conv_w, conv_b, down_w, down_b):
    nz, ny = lax.axis_size("gz"), lax.axis_size("gy")
    shapes = [
        ((OUT * 64, HX), bf16),
        ((C * NZ * NY, NX), f32),
        ((2, C * NY, NX), bf16),
        ((2, C * NZ, NX), bf16),
        ((4, 8, NX), f32),
        ((8, 512), f32),
        ((ny, 8, 384), f32),
    ]
    scratch = [
        ((C, NY, NX), bf16),
        ((C, NY, NX), bf16),
        ((C * NZ, NX), bf16),
        ((C * NZ, NX), bf16),
        ((4, 8, NX), f32),
        ((2, 2048, HX), f32),
        ((2, C * NZ, NX), bf16),
        ((4, 8, NX), f32),
        ((2, C * NY, NX), bf16),
        ((2, C * NZ, NX), bf16),
        ((4, 8, NX), f32),
        ((OUT, 512), f32),
        ((HID, 384), f32),
        ((nz, 8, 512), f32),
        ((ny, 8, 384), f32),
        ((8, 512), f32),
        ((8, 384), f32),
        ((ny, 8, 512), f32),
        ((nz, 8, 384), f32),
        ((8, 384), f32),
        ((NX, 4 * HX), bf16),
        ((256, 200), bf16),
        ((256, 256), bf16),
        ((TZ * TY * 32, HX), bf16),
        ((OUT * 64, HX), bf16),
        ((OUT * 64, HX), bf16),
        ((512, 512), bf16),
        ((384, 512), bf16),
        ((512, OUT), bf16),
        ((OUT, 512), bf16),
        ((4, 512, HX), f32),
        ((OUT, HX), f32),
        ((512, CELLS), f32),
        ((512, CELLS), f32),
        ((512, CELLS), bf16),
        ((512, CELLS), bf16),
        ((512, CELLS), f32),
        ((512, CELLS), f32),
        ((512, CELLS), bf16),
        ((4 * 512, HX), f32),
        ((TZ * TY * 24, HX), f32),
        ((OUT, HX), f32),
        ((OUT, HX), f32),
        ((32, HX), f32),
    ]
    return pl.pallas_call(
        functools.partial(compute_kernel, nz, ny),
        out_shape=[jax.ShapeDtypeStruct(s, d) for s, d in shapes],
        in_specs=[VMEM] * 6,
        out_specs=[VMEM] * 7,
        scratch_shapes=[pltpu.VMEM(s, d) for s, d in scratch]
        + [pltpu.SemaphoreType.DMA((2, 16 + 2 * nz + 3 * ny))],
        compiler_params=pltpu.CompilerParams(
            vmem_limit_bytes=60 * 2**20, collective_id=0, has_side_effects=True
        ),
        name="block",
    )(
        fields, target.reshape(OUT * 64, HX), conv_w, conv_b.reshape(1, HID),
        down_w, down_b.reshape(1, OUT),
    )


def finish_kernel(cells, sens, rz, ry, rc, gd, gc, sens_out, conv, cbias, down, dbias, loss):
    row = iota((NY, NX), 0)
    sides = [ry[0].astype(f32), ry[1].astype(f32)]
    for ch in range(C):
        for z in range(NZ):
            i = ch * NZ + z
            value = sens[i * NY : (i + 1) * NY, :]
            low, high = sides[0][i : i + 1], sides[1][i : i + 1]
            if z in (0, NZ - 1):
                side = 0 if z == 0 else 1
                value = value + rz[side, ch * NY : (ch + 1) * NY, :].astype(f32)
                low = low + rc[2 * side, ch : ch + 1, :]
                high = high + rc[2 * side + 1, ch : ch + 1, :]
            value = value + jnp.where(row == 0, low, 0.0)
            value = value + jnp.where(row == NY - 1, high, 0.0)
            sens_out[i * NY : (i + 1) * NY, :] = value
    total = gc[...].reshape(HID, 384)
    exact = functools.partial(
        lax.dot_general, dimension_numbers=NT, preferred_element_type=f32,
        precision=lax.Precision.HIGHEST,
    )
    scale = 1.0 / cells
    conv[...] = exact(total, tap_matrix(384)) * scale
    lane, r = iota((8, 384), 1), iota((8, 384), 0)
    pick = one_hot(lane == jnp.where(r == 0, 24, r + 27))
    rows = exact(pick, total) * scale
    cbias[...] = rows[0:1]
    dbias[...] = rows[1:3]
    down[...] = gd[...] * scale
    square = jnp.where(iota((HID, 384), 1) == 30, total, 0.0)
    loss[...] = jnp.sum(square, keepdims=True) * (scale / OUT)


def finish(sens, rz, ry, rc, gd, gc):
    cells = 64 * HX * lax.axis_size("gz") * lax.axis_size("gy")
    shapes = [sens.shape, (HID, C * 27), (1, HID), (8, 512), (2, HID), (1, 1)]
    return pl.pallas_call(
        functools.partial(finish_kernel, cells),
        out_shape=[jax.ShapeDtypeStruct(s, f32) for s in shapes],
        in_specs=[VMEM] * 6,
        out_specs=[VMEM] * 6,
        name="finish",
    )(sens, rz, ry, rc, gd, gc)


def on_device(fields, target, conv_w, conv_b, down_w, down_b):
    out, sens, rz, ry, rc, gd, gc = compute(fields, target, conv_w, conv_b, down_w, down_b)
    sens, conv, cbias, down, dbias, loss = finish(sens, rz, ry, rc, gd, gc)
    return (
        out.reshape(target.shape),
        sens.reshape(fields.shape),
        conv,
        cbias.reshape(HID),
        down,
        dbias.reshape(OUT),
        loss.reshape(()),
    )


def solution(mesh):
    block = P(None, "gz", "gy", None)
    return jax.shard_map(
        on_device,
        mesh=mesh,
        in_specs=(block, block, P(), P(), P(), P()),
        out_specs=(block, block, P(), P(), P("gz", None), P(), P()),
        check_vma=False,
    )
```
